32 devices in a mesh: dp: 16 (over z, y, core), fsdp: 2 (over x).
Axes of the slice: x: 2, y: 2, z: 4, core: 2. Of those that a mesh axis runs over, the one named last changes fastest.
Arguments:
- tokens: bfloat16 [16384, 1024], P(('dp', 'fsdp')), may hold values from -6 to 6
- lengths: int32 [64], P(('dp', 'fsdp')), may hold values from 32 to 256, as said below
- cotangent: bfloat16 [16384, 1024], P(('dp', 'fsdp')), may hold values from -6 to 6
- early_norm: bfloat16 [1024], P('fsdp'), may hold values from 0.25 to 1.75
- early_up: bfloat16 [1024, 4096], P(None, 'fsdp'), may hold values from -0.1875 to 0.1875
- early_down: bfloat16 [4096, 1024], P('fsdp'), may hold values from -0.09375 to 0.09375
- attend_norm: bfloat16 [1024], P('fsdp'), may hold values from 0.25 to 1.75
- heads_weight: bfloat16 [1024, 3072], P('fsdp'), may hold values from -0.1875 to 0.1875
- position_weight: bfloat16 [1024, 1024], P('fsdp'), may hold values from -0.1875 to 0.1875
- content_bias: bfloat16 [1024], P('fsdp'), may hold values from -3 to 3
- position_bias: bfloat16 [1024], P('fsdp'), may hold values from -3 to 3
- attend_output: bfloat16 [1024, 1024], P('fsdp'), may hold values from -0.75 to 0.75
- mixer_norm: bfloat16 [1024], P('fsdp'), may hold values from 0.25 to 1.75
- gating_weight: bfloat16 [1024, 2048], P('fsdp'), may hold values from -0.1875 to 0.1875
- depth_kernel: bfloat16 [5, 1024], P(None, 'fsdp'), may hold values from -2.5 to 2.5
- batch_gain: bfloat16 [1024], P('fsdp'), may hold values from 0.25 to 1.75
- batch_shift: bfloat16 [1024], P('fsdp'), may hold values from -3 to 3
- mixer_output: bfloat16 [1024, 1024], P('fsdp'), may hold values from -0.1875 to 0.1875
- late_norm: bfloat16 [1024], P('fsdp'), may hold values from 0.25 to 1.75
- late_up: bfloat16 [1024, 4096], P(None, 'fsdp'), may hold values from -0.1875 to 0.1875
- late_down: bfloat16 [4096, 1024], P('fsdp'), may hold values from -0.09375 to 0.09375
- final_gain: bfloat16 [1024], P('fsdp'), may hold values from 0.25 to 1.75
Outputs:
- out: bfloat16 [16384, 1024], P(('dp', 'fsdp'))
- grad_tokens: bfloat16 [16384, 1024], P(('dp', 'fsdp'))
- grad_early_norm: float32 [1024], P('fsdp')
- grad_early_up: float32 [1024, 4096], P(None, 'fsdp')
- grad_early_down: float32 [4096, 1024], P('fsdp')
- grad_attend_norm: float32 [1024], P('fsdp')
- grad_heads_weight: float32 [1024, 3072], P('fsdp')
- grad_position_weight: float32 [1024, 1024], P('fsdp')
- grad_content_bias: float32 [1024], P('fsdp')
- grad_position_bias: float32 [1024], P('fsdp')
- grad_attend_output: float32 [1024, 1024], P('fsdp')
- grad_mixer_norm: float32 [1024], P('fsdp')
- grad_gating_weight: float32 [1024, 2048], P('fsdp')
- grad_depth_kernel: float32 [5, 1024], P(None, 'fsdp')
- grad_batch_gain: float32 [1024], P('fsdp')
- grad_batch_shift: float32 [1024], P('fsdp')
- grad_mixer_output: float32 [1024, 1024], P('fsdp')
- grad_late_norm: float32 [1024], P('fsdp')
- grad_late_up: float32 [1024, 4096], P(None, 'fsdp')
- grad_late_down: float32 [4096, 1024], P('fsdp')
- grad_final_gain: float32 [1024], P('fsdp')
The draws below stay inside these ranges and needn't reach their ends.
Inputs may be any that keep to these rules, and one draw needn't show every extreme that they name: Utterance i fills the first lengths[i] frames of its slot; in every draw some utterance fills all 256 frames.
All inputs are finite; a program needn't handle non-finite values.
Results may differ from the reference program's by a relative error of at most 0.025.
Values may be sent and summed in bfloat16 or wider, within the bound.
No kernel may reach another device: no remote copies, remote signals or barrier semaphores. Data moves between devices by JAX's collectives and lax.ppermute only.
A program may use at most 320 MiB of HBM per device.

```python
import math
import jax
import jax.numpy as jnp
from jax import lax

D = 1024
HEADS = 8
HEAD_DIM = 128
FF = 4096
KERNEL = 5
SLOT = 256
ITEMS = 64
TOKENS = 16384


def draw_lengths(key, part):
    key_level, key_length, key_top = jax.random.split(key, 3)
    level = jax.random.randint(key_level, (ITEMS,), 1, 5)
    bucket_cap = SLOT * level // 4
    bucket_floor = bucket_cap // 2
    offset = jax.random.randint(key_length, (ITEMS,), 0, SLOT + 1)
    length = bucket_floor + offset % (bucket_cap - bucket_floor + 1)
    top_item = jax.random.randint(key_top, (), 0, ITEMS)
    return jnp.where(jnp.arange(ITEMS) == top_item, SLOT, length).astype(jnp.int32)


def levels(own_key, dims, shards, smallest, high):
    level, own = 1.0, jax.random.fold_in(own_key, 6)
    for position, shards_of in shards:
        heights = jnp.exp(jax.random.uniform(jax.random.fold_in(own, position), (shards_of,), jnp.float32, smallest / len(shards), high / len(shards)))
        level = level * jnp.repeat(heights, dims[position] // shards_of).reshape([-1 if axis == position else 1 for axis in range(len(dims))])
    return level


def normal_values(own_key, shape, scale, limit, cuts=(), held_as=jnp.bfloat16):
    loudness = levels(own_key, shape, cuts, -0.22, 0.18) if cuts else 1.0
    values = jax.random.normal(own_key, shape, jnp.float32) * scale * loudness
    return jnp.minimum(jnp.maximum(values, -limit), limit).astype(held_as)


def setup_inputs(seed: int = 0) -> dict:
    seeds = jax.random.split(jax.random.key(seed), 23)
    return {
        "tokens": normal_values(seeds[0], (TOKENS, D), 1.0, 6.0, ((0, 32),)),
        "lengths": draw_lengths(jax.random.fold_in(seeds[22], 71), 0),
        "cotangent": normal_values(seeds[2], (TOKENS, D), 1.0, 6.0, ((0, 32),)),
        "early_norm": jnp.clip(1.0 + 0.15 * jax.random.normal(seeds[3], (D,), jnp.float32), 0.25, 1.75).astype(jnp.bfloat16),
        "early_up": normal_values(seeds[4], (D, FF), D ** -0.5, 0.1875, ((1, 2),)),
        "early_down": normal_values(seeds[5], (FF, D), FF ** -0.5, 0.09375, ((0, 2),)),
        "attend_norm": jnp.clip(1.0 + 0.15 * jax.random.normal(seeds[6], (D,), jnp.float32), 0.25, 1.75).astype(jnp.bfloat16),
        "heads_weight": normal_values(seeds[7], (D, 3 * D), D ** -0.5, 0.1875, ((0, 2),)),
        "position_weight": normal_values(seeds[8], (D, D), D ** -0.5, 0.1875, ((0, 2),)),
        "content_bias": normal_values(seeds[9], (D,), 0.5, 3.0, ((0, 2),)),
        "position_bias": normal_values(seeds[10], (D,), 0.5, 3.0, ((0, 2),)),
        "attend_output": normal_values(seeds[11], (D, D), (D // 16) ** -0.5, 0.75, ((0, 2),)),
        "mixer_norm": jnp.clip(1.0 + 0.15 * jax.random.normal(seeds[12], (D,), jnp.float32), 0.25, 1.75).astype(jnp.bfloat16),
        "gating_weight": normal_values(seeds[13], (D, 2 * D), D ** -0.5, 0.1875, ((0, 2),)),
        "depth_kernel": normal_values(seeds[14], (KERNEL, D), KERNEL ** -0.5, 2.5, ((1, 2),)),
        "batch_gain": jnp.clip(1.0 + 0.15 * jax.random.normal(seeds[15], (D,), jnp.float32), 0.25, 1.75).astype(jnp.bfloat16),
        "batch_shift": normal_values(seeds[16], (D,), 0.5, 3.0, ((0, 2),)),
        "mixer_output": normal_values(seeds[17], (D, D), D ** -0.5, 0.1875, ((0, 2),)),
        "late_norm": jnp.clip(1.0 + 0.15 * jax.random.normal(seeds[18], (D,), jnp.float32), 0.25, 1.75).astype(jnp.bfloat16),
        "late_up": normal_values(seeds[19], (D, FF), D ** -0.5, 0.1875, ((1, 2),)),
        "late_down": normal_values(seeds[20], (FF, D), FF ** -0.5, 0.09375, ((0, 2),)),
        "final_gain": jnp.clip(1.0 + 0.15 * jax.random.normal(seeds[21], (D,), jnp.float32), 0.25, 1.75).astype(jnp.bfloat16),
    }


@jax.custom_vjp
def low(v):
    return lax.optimization_barrier(v.astype(jnp.bfloat16)).astype(jnp.float32)

@jax.custom_vjp
def low_back(v):
    return v

def low_keep(v):
    return (low(v), None)

def low_pass(kept, grad):
    return (grad,)

def back_keep(v):
    return (v, None)

def back_low(kept, grad):
    return (low(grad),)
low.defvjp(low_keep, low_pass)
low_back.defvjp(back_keep, back_low)

def matmul(left, right):
    return jnp.dot(left, right, precision=lax.Precision.HIGHEST, preferred_element_type=jnp.float32)

def contract(form, left, right):
    return jnp.einsum(form, left, right, precision=lax.Precision.HIGHEST, preferred_element_type=jnp.float32)

def layer_norm(signal, norm_gain):
    average = lax.optimization_barrier(jnp.mean(signal, axis=-1, keepdims=True))
    centred = signal - average
    spread = lax.optimization_barrier(jnp.mean(centred * centred, axis=-1, keepdims=True))
    return centred * lax.rsqrt(spread + 1e-05) * norm_gain

def gated_units(joined):
    half_width = joined.shape[-1] // 2
    return joined[:, :half_width] * jax.nn.sigmoid(joined[:, half_width:])

def depthwise(signal, kernel):
    kernel_taps = kernel.shape[0]
    left_pad = (kernel_taps - 1) // 2
    frames = signal.shape[0]
    padded = jnp.pad(signal, ((left_pad, kernel_taps - 1 - left_pad), (0, 0)))
    running = jnp.zeros_like(signal)
    for offset in range(kernel_taps):
        running = running + padded[offset:offset + frames] * kernel[offset]
    return running

def batch_moments(first, second, frames_total):
    average = first / frames_total
    spread = second / frames_total - average * average
    return (average, lax.rsqrt(spread + 1e-05))

def batch_apply(mixed, average, inv_scale, scale_gain, shift_bias):
    return (mixed - average) * inv_scale * scale_gain + shift_bias

def rel_shift(spanning):
    head_count, frames, span_width = spanning.shape
    flat = spanning.reshape(head_count, frames * span_width)
    flat = flat[:, frames - 1:frames - 1 + frames * (span_width - 1)]
    return flat.reshape(head_count, frames, span_width - 1)[:, :, :frames]

def sinusoid(frames, model_width):
    distance = (frames - 1 - jnp.arange(2 * frames - 1)).astype(jnp.float32)
    halves = model_width // 2
    frequency = jnp.exp(jnp.arange(halves).astype(jnp.float32) * (-2.0 * math.log(10000.0) / model_width))
    angles = distance[:, None] * frequency[None, :]
    return jnp.concatenate([jnp.sin(angles), jnp.cos(angles)], axis=1)

def feed_forward(signal, norm_gain, up_weight, down_weight):
    normed = low(layer_norm(signal, norm_gain))
    hidden = low_back(matmul(normed, up_weight))
    active = low(jax.nn.silu(hidden))
    return signal + 0.5 * low_back(matmul(active, down_weight))

def attend(relative, pieces):
    q_content, q_position, key_rows, value_rows, key_valid = pieces
    frames = key_rows.shape[0]
    head_shape = (frames, HEADS, HEAD_DIM)
    content = contract('ihd,jhd->hij', q_content.reshape(head_shape), key_rows.reshape(head_shape))
    spanning = contract('ihd,nhd->hin', q_position.reshape(head_shape), relative.reshape(2 * frames - 1, HEADS, HEAD_DIM))
    raw_scores = low_back(content + rel_shift(spanning)) * (1.0 / math.sqrt(HEAD_DIM))
    scores = jnp.where(key_valid[None, None, :], raw_scores, -1e+30)
    weighting = low(jax.nn.softmax(scores, axis=-1))
    context = contract('hij,jhd->ihd', weighting, value_rows.reshape(head_shape))
    return context.reshape(frames, HEADS * HEAD_DIM)

def attention(signal, norm_gain, heads_weight, position_weight, content_bias, position_bias, output_weight, key_valid, table):
    model_width = signal.shape[1]
    utterances = key_valid.shape[0]
    frames = key_valid.shape[1]
    normed = low(layer_norm(signal, norm_gain))
    joined = low_back(matmul(normed, heads_weight))
    queries = joined[:, :model_width]
    key_rows = low(joined[:, model_width:2 * model_width])
    value_rows = low(joined[:, 2 * model_width:])
    q_content = low(queries + content_bias)
    q_position = low(queries + position_bias)
    relative = low(low_back(matmul(low(table), position_weight)))

    def per_item(array):
        return array.reshape(utterances, frames, model_width)
    checked = jax.checkpoint(attend)
    context = lax.map(lambda pieces: checked(relative, pieces), (per_item(q_content), per_item(q_position), per_item(key_rows), per_item(value_rows), key_valid))
    context = low(low_back(context.reshape(utterances * frames, model_width)))
    return signal + low_back(matmul(context, output_weight))

def convolution(signal, norm_gain, gating_weight, depth_kernel, batch_gain, batch_shift, output_weight, frame_mask):
    model_width = signal.shape[1]
    normed = low(layer_norm(signal, norm_gain))
    joined = low_back(matmul(normed, gating_weight))
    gated = gated_units(joined) * frame_mask
    mixed = jax.vmap(depthwise, (0, None))(gated.reshape(-1, SLOT, model_width), depth_kernel).reshape(gated.shape)
    first = lax.optimization_barrier(jnp.sum(frame_mask * mixed, axis=0))
    second = lax.optimization_barrier(jnp.sum(frame_mask * mixed * mixed, axis=0))
    average, inv_scale = batch_moments(first, second, jnp.sum(frame_mask))
    active = low(jax.nn.silu(batch_apply(mixed, average, inv_scale, batch_gain, batch_shift)))
    return signal + low_back(matmul(active, output_weight))

def forward(signal, params, frame_mask, key_valid, table):
    early_norm, early_up, early_down, attend_norm, heads_weight, position_weight, content_bias, position_bias, attend_output, mixer_norm, gating_weight, depth_kernel, batch_gain, batch_shift, mixer_output, late_norm, late_up, late_down, final_gain = params
    after_early = feed_forward(signal, early_norm, early_up, early_down)
    after_attend = attention(after_early, attend_norm, heads_weight, position_weight, content_bias, position_bias, attend_output, key_valid, table)
    after_mixer = convolution(after_attend, mixer_norm, gating_weight, depth_kernel, batch_gain, batch_shift, mixer_output, frame_mask)
    after_late = feed_forward(after_mixer, late_norm, late_up, late_down)
    return layer_norm(after_late, final_gain)

def reference(tokens, lengths, cotangent, early_norm, early_up, early_down, attend_norm, heads_weight, position_weight, content_bias, position_bias, attend_output, mixer_norm, gating_weight, depth_kernel, batch_gain, batch_shift, mixer_output, late_norm, late_up, late_down, final_gain):
    key_valid = jnp.arange(SLOT, dtype=jnp.int32)[None, :] < lengths[:, None]
    frame_mask = key_valid.reshape(-1, 1).astype(jnp.float32)
    table = sinusoid(SLOT, D)
    params = tuple((weight.astype(jnp.float32) for weight in (early_norm, early_up, early_down, attend_norm, heads_weight, position_weight, content_bias, position_bias, attend_output, mixer_norm, gating_weight, depth_kernel, batch_gain, batch_shift, mixer_output, late_norm, late_up, late_down, final_gain)))
    output, pullback = jax.vjp(lambda signal, values: forward(signal, values, frame_mask, key_valid, table), tokens.astype(jnp.float32), params)
    grad_signal, weight_grads = pullback(cotangent.astype(jnp.float32) * frame_mask)
    return (output.astype(jnp.bfloat16), grad_signal.astype(jnp.bfloat16), weight_grads[0], weight_grads[1], weight_grads[2], weight_grads[3], weight_grads[4], weight_grads[5], weight_grads[6], weight_grads[7], weight_grads[8], weight_grads[9], weight_grads[10], weight_grads[11], weight_grads[12], weight_grads[13], weight_grads[14], weight_grads[15], weight_grads[16], weight_grads[17], weight_grads[18])
```

```python
import functools
import math

import jax
import jax.numpy as jnp
from jax import lax
from jax.experimental import pallas as pl
from jax.experimental.pallas import tpu as pltpu
from jax.sharding import Mesh
from jax.sharding import PartitionSpec as P

HEAD_DIM = 128
F32 = jnp.float32
BF16 = jnp.bfloat16
SWAP = ((0, 1), (1, 0))
Z_NEAR = ((0, 1), (1, 0), (2, 3), (3, 2))
Z_FAR = ((0, 2), (2, 0), (1, 3), (3, 1))
VMEM_LIMIT = 56 << 20


def product(form, left, right):
    return jnp.einsum(form, left, right, preferred_element_type=F32)


def rows_of(array, start, size):
    return lax.dynamic_slice_in_dim(array, start, size, 0)


def cols_of(array, start, size):
    return lax.dynamic_slice_in_dim(array, start, size, 1)


def normalise(signal):
    centred = signal - jnp.mean(signal, axis=-1, keepdims=True)
    inverse = lax.rsqrt(jnp.mean(centred * centred, axis=-1, keepdims=True) + 1e-05)
    return centred * inverse, inverse


def norm_backward(signal, gain, upstream):
    unit, inverse = normalise(signal)
    scaled = upstream * gain
    along = jnp.mean(scaled * unit, axis=-1, keepdims=True)
    grad = inverse * (scaled - jnp.mean(scaled, axis=-1, keepdims=True) - unit * along)
    return grad, jnp.sum(upstream * unit, axis=0)


def silu_slope(value):
    gate = jax.nn.sigmoid(value)
    return gate * (1.0 + value * (1.0 - gate))


def shifted(pieces, offset):
    frames = pieces.shape[1]
    if offset == 0:
        return pieces
    if offset > 0:
        return jnp.pad(pieces[:, offset:], ((0, 0), (0, offset), (0, 0)))
    return jnp.pad(pieces[:, : frames + offset], ((0, 0), (-offset, 0), (0, 0)))


def sinusoid(rows, frames, model_width):
    distance = (frames - 1 - jnp.arange(rows)).astype(F32)
    halves = model_width // 2
    frequency = jnp.exp(
        jnp.arange(halves).astype(F32) * (-2.0 * math.log(10000.0) / model_width)
    )
    angles = distance[:, None] * frequency[None, :]
    return jnp.concatenate([jnp.sin(angles), jnp.cos(angles)], axis=1)


def head_columns(h, base=0):
    return pl.ds(pl.multiple_of(base + h * HEAD_DIM, HEAD_DIM), HEAD_DIM)


def dot(left, right, dims):
    return lax.dot_general(left, right, (dims, ((), ())), preferred_element_type=F32)


def attend_forward_body(lengths, joined, biases, relative, context, probs):
    frames, width = context.shape
    length = lengths[pl.program_id(0)]
    scale = 1.0 / math.sqrt(HEAD_DIM)
    key_index = lax.broadcasted_iota(jnp.int32, (frames, frames), 1)

    def head(h, carry):
        at = head_columns(h)
        queries = joined[:, at]
        keys = joined[:, head_columns(h, width)].astype(BF16)
        values = joined[:, head_columns(h, 2 * width)].astype(BF16)
        q_content = (queries + biases[0:1, at]).astype(BF16)
        q_position = (queries + biases[1:2, at]).astype(BF16)
        content = dot(q_content, keys, ((1,), (1,)))
        spanning = dot(q_position, relative[:, at], ((1,), (1,)))
        spanning = pltpu.roll(spanning, frames + 1, 1, stride=1, stride_axis=0)[:, :frames]
        scores = jnp.where(key_index < length, (content + spanning) * scale, -1e30)
        weights = jnp.exp(scores - jnp.max(scores, axis=-1, keepdims=True))
        low = (weights / jnp.sum(weights, axis=-1, keepdims=True)).astype(BF16)
        probs[0, h] = low
        context[:, at] = dot(low, values, ((1,), (0,))).astype(BF16)
        return carry

    lax.fori_loop(0, width // HEAD_DIM, head, 0)


def attend_backward_body(
    joined, biases, relative, probs, grad_context, grad_joined, grad_relative, grad_biases
):
    frames, width = grad_context.shape
    scale = 1.0 / math.sqrt(HEAD_DIM)
    row = lax.broadcasted_iota(jnp.int32, (frames, frames), 0)
    column = lax.broadcasted_iota(jnp.int32, (frames, frames), 1)
    flip = jnp.where(row + column == frames - 1, 1.0, 0.0).astype(BF16)

    @pl.when(pl.program_id(0) == 0)
    def _():
        grad_relative[...] = jnp.zeros_like(grad_relative)
        grad_biases[...] = jnp.zeros_like(grad_biases)

    def head(h, carry):
        at = head_columns(h)
        queries = joined[:, at]
        keys = joined[:, head_columns(h, width)].astype(BF16)
        values = joined[:, head_columns(h, 2 * width)].astype(BF16)
        q_content = (queries + biases[0:1, at]).astype(BF16)
        q_position = (queries + biases[1:2, at]).astype(BF16)
        low = probs[0, h]
        weights = low.astype(F32)
        upstream = grad_context[:, at]
        grad_probs = dot(upstream, values, ((1,), (1,)))
        grad_values = dot(low, upstream, ((0,), (0,)))
        inner = jnp.sum(grad_probs * weights, axis=-1, keepdims=True)
        grad_raw = (weights * (grad_probs - inner) * scale).astype(BF16)
        grad_keys = dot(grad_raw, q_content, ((0,), (0,)))
        turned = dot(flip, grad_raw, ((1,), (0,))).astype(BF16)
        q_turned = dot(flip, q_position, ((1,), (0,))).astype(BF16)
        wide = jnp.concatenate([turned, jnp.zeros_like(turned)], axis=1)
        wide = pltpu.roll(wide, 0, 1, stride=1, stride_axis=0)
        grad_content = dot(turned, keys, ((1,), (0,)))
        grad_position = dot(wide, relative[:, at], ((1,), (0,)))
        grad_queries = (grad_content + grad_position).astype(BF16)
        grad_relative[:, at] += dot(wide, q_turned, ((0,), (0,)))
        grad_biases[0:1, at] += jnp.sum(grad_content, axis=0, keepdims=True)
        grad_biases[1:2, at] += jnp.sum(grad_position, axis=0, keepdims=True)
        grad_joined[:, at] = dot(flip, grad_queries, ((1,), (0,))).astype(BF16)
        grad_joined[:, head_columns(h, width)] = grad_keys.astype(BF16)
        grad_joined[:, head_columns(h, 2 * width)] = grad_values.astype(BF16)
        return carry

    lax.fori_loop(0, width // HEAD_DIM, head, 0)


def attend_forward(joined, biases, relative, lengths):
    utterances = lengths.shape[0]
    frames = joined.shape[0] // utterances
    width = relative.shape[1]
    heads = width // HEAD_DIM
    return pl.pallas_call(
        attend_forward_body,
        grid_spec=pltpu.PrefetchScalarGridSpec(
            num_scalar_prefetch=1,
            grid=(utterances,),
            in_specs=[
                pl.BlockSpec((frames, 3 * width), lambda u, n: (u, 0)),
                pl.BlockSpec((2, width), lambda u, n: (0, 0)),
                pl.BlockSpec((2 * frames, width), lambda u, n: (0, 0)),
            ],
            out_specs=[
                pl.BlockSpec((frames, width), lambda u, n: (u, 0)),
                pl.BlockSpec((1, heads, frames, frames), lambda u, n: (u, 0, 0, 0)),
            ],
        ),
        out_shape=[
            jax.ShapeDtypeStruct((utterances * frames, width), BF16),
            jax.ShapeDtypeStruct((utterances, heads, frames, frames), BF16),
        ],
        compiler_params=pltpu.CompilerParams(vmem_limit_bytes=VMEM_LIMIT),
        cost_estimate=pl.CostEstimate(
            flops=10 * utterances * frames * frames * width,
            bytes_accessed=joined.size * 4 + utterances * frames * width * 4,
            transcendentals=utterances * heads * frames * frames,
        ),
        name="attend_forward",
    )(lengths, joined, biases, relative)


def attend_backward(joined, biases, relative, probs, grad_context):
    utterances, heads, frames, _ = probs.shape
    width = relative.shape[1]
    return pl.pallas_call(
        attend_backward_body,
        grid=(utterances,),
        in_specs=[
            pl.BlockSpec((frames, 3 * width), lambda u: (u, 0)),
            pl.BlockSpec((2, width), lambda u: (0, 0)),
            pl.BlockSpec((2 * frames, width), lambda u: (0, 0)),
            pl.BlockSpec((1, heads, frames, frames), lambda u: (u, 0, 0, 0)),
            pl.BlockSpec((frames, width), lambda u: (u, 0)),
        ],
        out_specs=[
            pl.BlockSpec((frames, 3 * width), lambda u: (u, 0)),
            pl.BlockSpec((2 * frames, width), lambda u: (0, 0)),
            pl.BlockSpec((2, width), lambda u: (0, 0)),
        ],
        out_shape=[
            jax.ShapeDtypeStruct((utterances * frames, 3 * width), BF16),
            jax.ShapeDtypeStruct((2 * frames, width), F32),
            jax.ShapeDtypeStruct((2, width), F32),
        ],
        compiler_params=pltpu.CompilerParams(vmem_limit_bytes=VMEM_LIMIT),
        cost_estimate=pl.CostEstimate(
            flops=24 * utterances * frames * frames * width,
            bytes_accessed=joined.size * 8,
            transcendentals=0,
        ),
        name="attend_backward",
    )(joined, biases, relative, probs, grad_context)


def place_body(count, block_rows, where, *refs):
    sources, target, held, arrived, left = refs[:count], refs[count], *refs[count + 1 :]
    copies = []
    for source in sources:
        for block in range(source.shape[0] // block_rows):
            slot = len(copies)
            start = pl.multiple_of(where[slot] * block_rows, block_rows)
            rows = pl.ds(slot * block_rows, block_rows)
            copies.append(
                (
                    pltpu.make_async_copy(
                        source.at[pl.ds(block * block_rows, block_rows)],
                        held.at[rows],
                        arrived.at[slot],
                    ),
                    pltpu.make_async_copy(
                        held.at[rows], target.at[pl.ds(start, block_rows)], left.at[slot]
                    ),
                )
            )
    for fetch, _ in copies:
        fetch.start()
    for fetch, store in copies:
        fetch.wait()
        store.start()
    for _, store in copies:
        store.wait()


def place(sources, block_rows, where, rows):
    blocks = rows // block_rows
    width = sources[0].shape[1]
    return pl.pallas_call(
        functools.partial(place_body, len(sources), block_rows),
        grid_spec=pltpu.PrefetchScalarGridSpec(
            num_scalar_prefetch=1,
            grid=(1,),
            in_specs=[pl.BlockSpec(memory_space=pl.ANY)] * len(sources),
            out_specs=pl.BlockSpec(memory_space=pl.ANY),
            scratch_shapes=[
                pltpu.VMEM((rows, width), sources[0].dtype),
                pltpu.SemaphoreType.DMA((blocks,)),
                pltpu.SemaphoreType.DMA((blocks,)),
            ],
        ),
        out_shape=jax.ShapeDtypeStruct((rows, width), sources[0].dtype),
        compiler_params=pltpu.CompilerParams(vmem_limit_bytes=VMEM_LIMIT),
        cost_estimate=pl.CostEstimate(
            flops=0, bytes_accessed=4 * rows * width, transcendentals=0
        ),
        name="place",
    )(where, *sources)


def widen_body(spans, by_rows, where, *refs):
    count = len(spans)
    sources, targets = refs[:4], refs[4 : 4 + count]
    held, wide, arrived, left = refs[4 + count :]
    rows = held.shape[1]
    block = rows // 4
    fetches = [
        pltpu.make_async_copy(sources[k], held.at[k], arrived.at[k]) for k in range(4)
    ]
    for fetch in fetches:
        fetch.start()
    stores = []
    for k in range(4):
        fetches[k].wait()
        for b in range(4):
            at = pl.ds(k * rows + b * block, block)
            wide[at, :] = held[k, b * block : (b + 1) * block].astype(F32)
            spot = where[4 * k + b]
            for n, ((start, span), target) in enumerate(zip(spans, targets)):
                if by_rows:
                    into = target.at[pl.ds(pl.multiple_of(spot * block, block), block)]
                else:
                    row = pl.multiple_of(lax.rem(spot, 8) * block, block)
                    column = pl.multiple_of((spot // 8) * span, HEAD_DIM)
                    into = target.at[pl.ds(row, block), pl.ds(column, span)]
                store = pltpu.make_async_copy(
                    wide.at[at, pl.ds(start, span)], into, left.at[len(stores)]
                )
                store.start()
                stores.append(store)
    for store in stores:
        store.wait()


def widen(sources, spans, where, by_rows):
    rows, width = sources[0].shape
    if by_rows:
        shards = [jax.ShapeDtypeStruct((4 * rows, span), F32) for _, span in spans]
    else:
        shards = [jax.ShapeDtypeStruct((2 * rows, 2 * span), F32) for _, span in spans]
    return pl.pallas_call(
        functools.partial(widen_body, spans, by_rows),
        grid_spec=pltpu.PrefetchScalarGridSpec(
            num_scalar_prefetch=1,
            grid=(1,),
            in_specs=[pl.BlockSpec(memory_space=pl.ANY)] * 4,
            out_specs=[pl.BlockSpec(memory_space=pl.ANY)] * len(spans),
            scratch_shapes=[
                pltpu.VMEM((4, rows, width), BF16),
                pltpu.VMEM((4 * rows, width), F32),
                pltpu.SemaphoreType.DMA((4,)),
                pltpu.SemaphoreType.DMA((16 * len(spans),)),
            ],
        ),
        out_shape=shards,
        compiler_params=pltpu.CompilerParams(vmem_limit_bytes=VMEM_LIMIT),
        cost_estimate=pl.CostEstimate(
            flops=0, bytes_accessed=4 * rows * width * 6, transcendentals=0
        ),
        name="widen",
    )(where, *sources)


class PairPlan:
    axes = ("z", "y", "c", "x")

    def __init__(self):
        self.z, self.y, self.c, self.x = (lax.axis_index(name) for name in self.axes)
        self.near = lax.rem(self.z, 2)
        self.far = self.z // 2

    def over(self, name, value):
        return lax.ppermute(value, name, SWAP)

    def over_near(self, value):
        return lax.ppermute(value, "z", Z_NEAR)

    def over_far(self, value):
        return lax.ppermute(value, "z", Z_FAR)

    def total(self, value):
        value = value + self.over("c", value)
        diagonal = ((0, 3), (3, 0), (1, 2), (2, 1))
        value = (value + self.over("x", value)) + (
            self.over("y", value) + lax.ppermute(value, ("y", "x"), diagonal)
        )
        turned = [
            lax.ppermute(value, "z", tuple((i, (i + k) % 4) for i in range(4))) for k in (1, 2, 3)
        ]
        return (value + turned[1]) + (turned[0] + turned[2])

    def whole_vectors(self, stacked):
        other = self.over("x", stacked)
        low = jnp.where(self.x == 0, stacked, other)
        high = jnp.where(self.x == 0, other, stacked)
        return jnp.concatenate([low, high], axis=1)

    def fetch(self, shard, y_first):
        eighth = shard.shape[0] // 8
        mine = self.c * 4 + self.y * 2 + self.near
        piece = self.over("x", rows_of(shard, mine * eighth, eighth))
        if y_first:
            both = jnp.concatenate([piece, self.over("y", piece)], axis=0)
            others = self.over_near(both)
            flips = (0, 2, 1, 3)
        else:
            both = jnp.concatenate([piece, self.over_near(piece)], axis=0)
            others = self.over("y", both)
            flips = (0, 1, 2, 3)
        sources = (both, others, self.over("c", both), self.over("c", others))
        inner = self.y * 2 + self.near
        places = [jnp.bitwise_xor(inner, flip) for flip in flips]
        places = [self.c * 4 + k for k in places] + [(1 - self.c) * 4 + k for k in places]
        return sources, places, eighth

    def other_shard(self, shard, y_first):
        sources, places, eighth = self.fetch(shard, y_first)
        return place(sources, eighth, jnp.stack(places), shard.shape[0])

    def whole_rows(self, shard, y_first):
        sources, places, eighth = self.fetch(shard, y_first)
        places = [(1 - self.x) * 8 + k for k in places] + [self.x * 8 + k for k in range(8)]
        return place(sources + (shard,), eighth, jnp.stack(places), 2 * shard.shape[0])

    def pairs(self, up, down):
        return [(up, down), (self.other_shard(up, True), self.other_shard(down, False))]

    def with_core(self, value):
        return jnp.concatenate([value, self.over("c", value)], axis=0)

    def with_core_half(self, value):
        half = value.shape[1] // 2
        sent = self.over("c", cols_of(value, (1 - self.c) * half, half))
        return jnp.concatenate([cols_of(value, self.c * half, half), sent], axis=0)

    def summed(self, keep, send, spans, by_rows):
        half = keep.shape[0] // 2
        quarter, eighth = half // 2, half // 4

        def cut(value, start, size):
            return rows_of(value, start, size).astype(F32)

        met = self.over("x", send)
        away = (1 - self.y) * half
        sent = (cut(keep, away, half) + cut(met, away, half)).astype(BF16)
        mine = cut(keep, self.y * half, half) + cut(met, self.y * half, half)
        mine = mine + self.over("y", sent).astype(F32)
        sent = rows_of(mine, (1 - self.near) * quarter, quarter).astype(BF16)
        mine = rows_of(mine, self.near * quarter, quarter) + self.over_near(sent).astype(F32)
        sent = rows_of(mine, (1 - self.far) * eighth, eighth).astype(BF16)
        mine = rows_of(mine, self.far * eighth, eighth) + self.over_far(sent).astype(F32)
        mine = mine.astype(BF16)
        line = jnp.concatenate([mine, self.over_far(mine)], axis=0)
        line = jnp.concatenate([line, self.over_near(line)], axis=0)
        other = self.over("y", line)
        sources = (line, other, self.over("c", line), self.over("c", other))
        places = []
        for c in (self.c, 1 - self.c):
            for y in (self.y, 1 - self.y):
                for near in (self.near, 1 - self.near):
                    for far in (self.far, 1 - self.far):
                        places.append(c * 8 + y * 4 + near * 2 + far)
        return widen(sources, spans, jnp.stack(places), by_rows)


def split_sizes(array, sizes):
    out, start = [], 0
    for size in sizes:
        out.append(array[:, start : start + size])
        start += size
    return out


def pair_layer(*arguments):
    (
        tokens,
        lengths,
        cotangent,
        early_norm,
        early_up,
        early_down,
        attend_norm,
        heads_weight,
        position_weight,
        content_bias,
        position_bias,
        attend_output,
        mixer_norm,
        gating_weight,
        depth_kernel,
        batch_gain,
        batch_shift,
        mixer_output,
        late_norm,
        late_up,
        late_down,
        final_gain,
    ) = arguments
    plan = PairPlan()
    utterances = lengths.shape[0]
    rows, width = tokens.shape
    frames = rows // utterances
    taps = depth_kernel.shape[0]
    middle = (taps - 1) // 2
    mask = (lax.iota(jnp.int32, frames)[None, :] < lengths[:, None]).reshape(rows, 1).astype(F32)

    early = plan.pairs(early_up, early_down)
    vectors = jnp.stack(
        [
            early_norm,
            attend_norm,
            mixer_norm,
            late_norm,
            final_gain,
            content_bias,
            position_bias,
            batch_gain,
            batch_shift,
        ]
    )
    vectors = plan.whole_vectors(jnp.concatenate([vectors, depth_kernel], axis=0)).astype(F32)
    early_norm, attend_norm, mixer_norm, late_norm, final_gain = vectors[0:5]
    biases = vectors[5:7]
    batch_gain, batch_shift = vectors[7:9]
    depth_kernel = vectors[9:]
    attend_packed = plan.whole_rows(
        jnp.concatenate([heads_weight, position_weight, attend_output], axis=1), True
    )
    heads_weight, position_weight, attend_output = split_sizes(
        attend_packed, (3 * width, width, width)
    )
    mixer_packed = plan.whole_rows(jnp.concatenate([gating_weight, mixer_output], axis=1), False)
    gating_weight, mixer_output = split_sizes(mixer_packed, (2 * width, width))
    late = plan.pairs(late_up, late_down)

    def ffn_forward(signal, gain, parts):
        normed = (normalise(signal)[0] * gain).astype(BF16)
        hidden = [product("td,df->tf", normed, up) for up, _ in parts]
        active = [jax.nn.silu(value).astype(BF16) for value in hidden]
        total = sum(product("tf,fd->td", a, down) for a, (_, down) in zip(active, parts))
        return signal + 0.5 * total, (signal, normed, hidden, active)

    def ffn_backward(saved, gain, parts, upstream):
        signal, normed, hidden, active = saved
        out_grad = (0.5 * upstream).astype(BF16)
        grad_hidden = [
            (product("td,fd->tf", out_grad, down) * silu_slope(value)).astype(BF16)
            for value, (_, down) in zip(hidden, parts)
        ]
        both_out = plan.with_core(out_grad)
        grad_downs = [
            product("tf,td->fd", plan.with_core_half(a), both_out).astype(BF16) for a in active
        ]
        grad_downs, grad_hidden = lax.optimization_barrier((grad_downs, grad_hidden))
        down_shard = plan.summed(grad_downs[0], grad_downs[1], ((0, width),), True)[0]
        both_normed = plan.with_core(normed)
        grad_ups = [
            product("td,tf->df", both_normed, plan.with_core_half(g)).astype(BF16)
            for g in grad_hidden
        ]
        grad_ups, grad_hidden = lax.optimization_barrier((grad_ups, grad_hidden))
        half = grad_ups[0].shape[1]
        up_shard = plan.summed(grad_ups[0], grad_ups[1], ((0, half),), False)[0]
        grad_normed = sum(product("tf,df->td", g, up) for g, (up, _) in zip(grad_hidden, parts))
        grad_signal, grad_gain = norm_backward(signal, gain, grad_normed)
        return upstream + grad_signal, grad_gain, up_shard, down_shard

    start = tokens.astype(F32)
    after_early, early_saved = ffn_forward(start, early_norm, early)

    att_normed = (normalise(after_early)[0] * attend_norm).astype(BF16)
    joined = product("td,de->te", att_normed, heads_weight)
    table = sinusoid(2 * frames, frames, width).astype(BF16)
    relative = product("nc,cd->nd", table, position_weight).astype(BF16)
    context, probs = attend_forward(joined, biases, relative, lengths)
    after_attend = after_early + product("td,de->te", context, attend_output)

    mix_normed = (normalise(after_attend)[0] * mixer_norm).astype(BF16)
    gate_joined = product("td,de->te", mix_normed, gating_weight)
    linear, gate = gate_joined[:, :width], jax.nn.sigmoid(gate_joined[:, width:])
    slots = (utterances, frames, width)
    gated = (linear * gate * mask).reshape(slots)
    mixed = sum(shifted(gated, k - middle) * depth_kernel[k] for k in range(taps))
    mixed = mixed.reshape(rows, width)
    masked = mixed * mask
    counts = jnp.full((1, width), 1.0, F32) * jnp.sum(mask)
    moments = jnp.concatenate(
        [
            jnp.sum(masked, axis=0, keepdims=True),
            jnp.sum(masked * mixed, axis=0, keepdims=True),
            counts,
        ],
        axis=0,
    )
    moments = plan.total(moments)
    frames_total = moments[2]
    average = moments[0] / frames_total
    inv_scale = lax.rsqrt(moments[1] / frames_total - average * average + 1e-05)
    bn_out = (mixed - average) * inv_scale * batch_gain + batch_shift
    mix_active = jax.nn.silu(bn_out).astype(BF16)
    after_mixer = after_attend + product("td,de->te", mix_active, mixer_output)

    after_late, late_saved = ffn_forward(after_mixer, late_norm, late)
    unit, _ = normalise(after_late)
    output = (unit * final_gain).astype(BF16)

    upstream, grad_final = norm_backward(
        after_late, final_gain, cotangent.astype(F32) * mask
    )
    upstream, grad_late_norm, late_up_shard, late_down_shard = ffn_backward(
        late_saved, late_norm, late, upstream
    )

    mix_out_grad = upstream.astype(BF16)
    grad_bn = product("te,de->td", mix_out_grad, mixer_output) * silu_slope(bn_out)
    unit_mixed = (mixed - average) * inv_scale
    bn_sums = plan.total(
        jnp.stack([jnp.sum(grad_bn * unit_mixed, axis=0), jnp.sum(grad_bn, axis=0)])
    )
    grad_gain, grad_shift = bn_sums[0], bn_sums[1]
    grad_average = -grad_shift * inv_scale * batch_gain
    grad_inv = grad_gain * batch_gain / inv_scale
    sec_grad = -0.5 * inv_scale * inv_scale * inv_scale * grad_inv / frames_total
    first_grad = grad_average / frames_total - 2.0 * average * sec_grad
    grad_mixed = grad_bn * inv_scale * batch_gain + mask * (first_grad + 2.0 * mixed * sec_grad)
    grad_mixed = grad_mixed.reshape(slots)
    grad_gated = sum(shifted(grad_mixed, middle - k) * depth_kernel[k] for k in range(taps))
    grad_depth = [
        jnp.sum(grad_mixed * shifted(gated, k - middle), axis=(0, 1)) for k in range(taps)
    ]
    grad_gated = grad_gated.reshape(rows, width) * mask
    grad_gate_joined = jnp.concatenate(
        [grad_gated * gate, grad_gated * linear * gate * (1.0 - gate)], axis=1
    ).astype(BF16)
    half = width // 2
    mix_half = plan.with_core_half(mix_out_grad)
    both_active = plan.with_core(mix_active)
    both_mix = plan.with_core(mix_normed)
    gate_half = plan.with_core_half(grad_gate_joined)
    mixer_blocks = jnp.concatenate(
        [product("td,te->de", both_mix, gate_half), product("td,te->de", both_active, mix_half)],
        axis=1,
    ).astype(BF16)
    mixer_blocks, grad_gate_joined = lax.optimization_barrier((mixer_blocks, grad_gate_joined))
    gating_shard, mixer_output_shard = plan.summed(
        rows_of(mixer_blocks, plan.x * half, half),
        rows_of(mixer_blocks, (1 - plan.x) * half, half),
        ((0, width), (width, half)),
        False,
    )
    grad_normed = product("te,de->td", grad_gate_joined, gating_weight)
    grad_signal, grad_mixer_norm = norm_backward(after_attend, mixer_norm, grad_normed)
    upstream = upstream + grad_signal

    att_out_grad = upstream.astype(BF16)
    grad_context = product("te,de->td", att_out_grad, attend_output).astype(BF16)
    grad_joined, grad_relative, grad_biases = attend_backward(
        joined, biases, relative, probs, grad_context
    )
    grad_relative = grad_relative.astype(BF16)
    relative_half = cols_of(grad_relative, plan.c * half, half).astype(F32) + plan.over(
        "c", cols_of(grad_relative, (1 - plan.c) * half, half)
    ).astype(F32)
    attend_blocks = jnp.concatenate(
        [
            product("td,te->de", plan.with_core(att_normed), plan.with_core_half(grad_joined)),
            product("nc,nd->cd", table, relative_half.astype(BF16)),
            product("td,te->de", plan.with_core(context), plan.with_core_half(att_out_grad)),
        ],
        axis=1,
    ).astype(BF16)
    attend_blocks, grad_joined = lax.optimization_barrier((attend_blocks, grad_joined))
    heads_shard, position_shard, attend_output_shard = plan.summed(
        rows_of(attend_blocks, plan.x * half, half),
        rows_of(attend_blocks, (1 - plan.x) * half, half),
        ((0, 3 * half), (3 * half, half), (4 * half, half)),
        False,
    )
    grad_normed = product("te,de->td", grad_joined, heads_weight)
    grad_signal, grad_attend_norm = norm_backward(after_early, attend_norm, grad_normed)
    upstream = upstream + grad_signal

    upstream, grad_early_norm, early_up_shard, early_down_shard = ffn_backward(
        early_saved, early_norm, early, upstream
    )
    small = jnp.stack(
        [
            grad_early_norm,
            grad_attend_norm,
            grad_biases[0],
            grad_biases[1],
            grad_mixer_norm,
            grad_late_norm,
            grad_final,
        ]
        + grad_depth
    )
    small = plan.total(small)
    small = cols_of(jnp.concatenate([small, bn_sums], axis=0), plan.x * half, half)
    return (
        output,
        upstream.astype(BF16),
        small[0],
        early_up_shard,
        early_down_shard,
        small[1],
        heads_shard,
        position_shard,
        small[2],
        small[3],
        attend_output_shard,
        small[4],
        gating_shard,
        small[7 : 7 + taps],
        small[7 + taps],
        small[8 + taps],
        mixer_output_shard,
        small[5],
        late_up_shard,
        late_down_shard,
        small[6],
    )


def layer_norm(signal, norm_gain):
    average = jnp.mean(signal, axis=-1, keepdims=True)
    centred = signal - average
    spread = jnp.mean(centred * centred, axis=-1, keepdims=True)
    return centred * lax.rsqrt(spread + 1e-05) * norm_gain


def gated_units(joined):
    half_width = joined.shape[-1] // 2
    return joined[:, :half_width] * jax.nn.sigmoid(joined[:, half_width:])


def depthwise(signal, kernel):
    kernel_taps = kernel.shape[0]
    left_pad = (kernel_taps - 1) // 2
    frames = signal.shape[0]
    padded = jnp.pad(signal, ((left_pad, kernel_taps - 1 - left_pad), (0, 0)))
    running = jnp.zeros_like(signal)
    for offset in range(kernel_taps):
        running = running + padded[offset : offset + frames] * kernel[offset]
    return running


def slot_conv(signal, kernel, frames):
    model_width = signal.shape[1]
    pieces = signal.reshape(-1, frames, model_width)
    return jax.vmap(depthwise, (0, None))(pieces, kernel).reshape(signal.shape)


def batch_moments(first, second, frames_total):
    average = first / frames_total
    spread = second / frames_total - average * average
    return (average, lax.rsqrt(spread + 1e-05))


def batch_apply(mixed, average, inv_scale, scale_gain, shift_bias):
    return (mixed - average) * inv_scale * scale_gain + shift_bias


def rel_shift(spanning):
    head_count, frames, span_width = spanning.shape
    flat = spanning.reshape(head_count, frames * span_width)
    flat = flat[:, frames - 1 : frames - 1 + frames * (span_width - 1)]
    return flat.reshape(head_count, frames, span_width - 1)[:, :, :frames]


def distances(frames, model_width):
    distance = (frames - 1 - jnp.arange(2 * frames - 1)).astype(jnp.float32)
    halves = model_width // 2
    frequency = jnp.exp(
        jnp.arange(halves).astype(jnp.float32) * (-2.0 * math.log(10000.0) / model_width)
    )
    angles = distance[:, None] * frequency[None, :]
    return jnp.concatenate([jnp.sin(angles), jnp.cos(angles)], axis=1)


def prepare_ffn(norm_gain, up_weight, down_weight):
    return (
        lax.all_gather(norm_gain, "fsdp", axis=0, tiled=True),
        lax.all_gather(up_weight, "fsdp", axis=1, tiled=True),
        lax.all_gather(down_weight, "fsdp", axis=0, tiled=True),
    )


def gather_attend(
    norm_gain, heads_weight, position_weight, content_bias, position_bias, output_weight, final_gain
):
    return (
        lax.all_gather(norm_gain, "fsdp", axis=0, tiled=True),
        lax.all_gather(heads_weight, "fsdp", axis=0, tiled=True),
        lax.all_gather(position_weight, "fsdp", axis=0, tiled=True),
        lax.all_gather(content_bias, "fsdp", axis=0, tiled=True),
        lax.all_gather(position_bias, "fsdp", axis=0, tiled=True),
        lax.all_gather(output_weight, "fsdp", axis=0, tiled=True),
        lax.all_gather(final_gain, "fsdp", axis=0, tiled=True),
    )


def gather_mixer(norm_gain, gating_weight, depth_kernel, batch_gain, batch_shift, output_weight):
    return (
        lax.all_gather(norm_gain, "fsdp", axis=0, tiled=True),
        lax.all_gather(gating_weight, "fsdp", axis=0, tiled=True),
        lax.all_gather(depth_kernel, "fsdp", axis=1, tiled=True),
        lax.all_gather(batch_gain, "fsdp", axis=0, tiled=True),
        lax.all_gather(batch_shift, "fsdp", axis=0, tiled=True),
        lax.all_gather(output_weight, "fsdp", axis=0, tiled=True),
    )


def ffn_forward(signal, weights):
    norm_gain, up_weight, down_weight = weights
    normed = layer_norm(signal, norm_gain.astype(jnp.float32)).astype(jnp.bfloat16)
    hidden = product("td,df->tf", normed, up_weight)
    active = jax.nn.silu(hidden).astype(jnp.bfloat16)
    return signal + 0.5 * product("tf,fd->td", active, down_weight)


def ffn_backward(signal, weights, upstream):
    norm_gain, up_weight, down_weight = weights
    normed_full, norm_pull = jax.vjp(layer_norm, signal, norm_gain.astype(jnp.float32))
    normed = normed_full.astype(jnp.bfloat16)
    out_grad = (0.5 * upstream).astype(jnp.bfloat16)
    hidden = product("td,df->tf", normed, up_weight)
    active_full, silu_pull = jax.vjp(jax.nn.silu, hidden)
    active = active_full.astype(jnp.bfloat16)
    grad_down = product("tf,td->fd", active, out_grad)
    grad_active = product("td,fd->tf", out_grad, down_weight)
    grad_hidden = silu_pull(grad_active)[0].astype(jnp.bfloat16)
    grad_up = product("td,tf->df", normed, grad_hidden)
    grad_normed = product("tf,df->td", grad_hidden, up_weight)
    grad_signal, grad_gain = norm_pull(grad_normed)
    shards = (
        lax.psum_scatter(
            grad_gain.astype(jnp.bfloat16), "fsdp", scatter_dimension=0, tiled=True
        ).astype(jnp.float32),
        lax.psum_scatter(
            grad_up.astype(jnp.bfloat16), "fsdp", scatter_dimension=1, tiled=True
        ).astype(jnp.float32),
        lax.psum_scatter(
            grad_down.astype(jnp.bfloat16), "fsdp", scatter_dimension=0, tiled=True
        ).astype(jnp.float32),
    )
    return (upstream + grad_signal, shards)


def attend_block(signal, weights, key_valid, table, upstream):
    (
        norm_gain,
        heads_weight,
        position_weight,
        content_bias,
        position_bias,
        output_weight,
        final_gain,
    ) = weights
    utterances, frames = key_valid.shape
    rows_total, model_width = signal.shape
    head_count = model_width // HEAD_DIM
    head_shape = (utterances, frames, head_count, HEAD_DIM)
    score_scale = 1.0 / math.sqrt(HEAD_DIM)
    normed_full, norm_pull = jax.vjp(layer_norm, signal, norm_gain.astype(jnp.float32))
    normed = normed_full.astype(jnp.bfloat16)
    joined = product("td,de->te", normed, heads_weight)
    queries = joined[:, :model_width]
    key_rows = joined[:, model_width : 2 * model_width].astype(jnp.bfloat16).reshape(head_shape)
    value_rows = joined[:, 2 * model_width :].astype(jnp.bfloat16).reshape(head_shape)
    q_content = (
        (queries + content_bias.astype(jnp.float32)).astype(jnp.bfloat16).reshape(head_shape)
    )
    q_position = (
        (queries + position_bias.astype(jnp.float32)).astype(jnp.bfloat16).reshape(head_shape)
    )
    relative = product("nc,cd->nd", table, position_weight).astype(jnp.bfloat16)
    relative = relative.reshape(2 * frames - 1, head_count, HEAD_DIM)
    content = product("uihd,ujhd->uhij", q_content, key_rows)
    shifted, shift_pull = jax.vjp(
        jax.vmap(rel_shift), product("uihd,nhd->uhin", q_position, relative)
    )
    scores = jnp.where(key_valid[:, None, None, :], (content + shifted) * score_scale, -1e30)
    weighting = jax.nn.softmax(scores, axis=-1)
    weighting_low = weighting.astype(jnp.bfloat16)
    context = product("uhij,ujhd->uihd", weighting_low, value_rows).reshape(rows_total, model_width)
    context = context.astype(jnp.bfloat16)
    if upstream is None:
        return signal + product("td,de->te", context, output_weight)
    out_grad = upstream.astype(jnp.bfloat16)
    grad_output = product("td,te->de", context, out_grad)
    grad_context = (
        product("te,de->td", out_grad, output_weight).astype(jnp.bfloat16).reshape(head_shape)
    )
    grad_weighting = product("uihd,ujhd->uhij", grad_context, value_rows)
    grad_values = product("uhij,uihd->ujhd", weighting_low, grad_context)
    grad_scores = weighting * (
        grad_weighting - jnp.sum(grad_weighting * weighting, axis=-1, keepdims=True)
    )
    grad_raw = (grad_scores * score_scale).astype(jnp.bfloat16)
    grad_q_content = product("uhij,ujhd->uihd", grad_raw, key_rows)
    grad_keys = product("uhij,uihd->ujhd", grad_raw, q_content)
    grad_spanning = shift_pull(grad_raw.astype(jnp.float32))[0].astype(jnp.bfloat16)
    grad_q_position = product("uhin,nhd->uihd", grad_spanning, relative)
    grad_relative = product("uhin,uihd->nhd", grad_spanning, q_position)
    grad_relative = grad_relative.reshape(2 * frames - 1, model_width).astype(jnp.bfloat16)
    grad_position = product("nc,nd->cd", table, grad_relative)
    grad_content_bias = jnp.sum(grad_q_content, axis=(0, 1)).reshape(model_width)
    grad_position_bias = jnp.sum(grad_q_position, axis=(0, 1)).reshape(model_width)
    grad_joined = jnp.concatenate(
        [
            (grad_q_content + grad_q_position).reshape(rows_total, model_width),
            grad_keys.reshape(rows_total, model_width),
            grad_values.reshape(rows_total, model_width),
        ],
        axis=1,
    ).astype(jnp.bfloat16)
    grad_heads = product("td,te->de", normed, grad_joined)
    grad_normed = product("te,de->td", grad_joined, heads_weight)
    grad_signal, grad_gain = norm_pull(grad_normed)
    return (
        upstream + grad_signal,
        (grad_gain, grad_heads, grad_position, grad_content_bias, grad_position_bias, grad_output),
    )


def mixer_block(signal, weights, frame_mask, frames, totals, upstream):
    norm_gain, gating_weight, depth_kernel, batch_gain, batch_shift, output_weight = weights
    normed_full, norm_pull = jax.vjp(layer_norm, signal, norm_gain.astype(jnp.float32))
    normed = normed_full.astype(jnp.bfloat16)
    joined = product("td,de->te", normed, gating_weight)
    gated, gate_pull = jax.vjp(gated_units, joined)
    mixed, conv_pull = jax.vjp(
        lambda values, taps: slot_conv(values, taps, frames),
        gated * frame_mask,
        depth_kernel.astype(jnp.float32),
    )
    if totals is None:
        totals = lax.psum(
            (
                jnp.sum(frame_mask * mixed, axis=0),
                jnp.sum(frame_mask * mixed * mixed, axis=0),
                jnp.sum(frame_mask),
            ),
            ("dp", "fsdp"),
        )
    first, second, frames_total = totals
    moments, moment_pull = jax.vjp(
        lambda summed_first, summed_second: batch_moments(
            summed_first, summed_second, frames_total
        ),
        first,
        second,
    )
    bn_out, apply_pull = jax.vjp(
        batch_apply,
        mixed,
        moments[0],
        moments[1],
        batch_gain.astype(jnp.float32),
        batch_shift.astype(jnp.float32),
    )
    active_full, silu_pull = jax.vjp(jax.nn.silu, bn_out)
    active = active_full.astype(jnp.bfloat16)
    if upstream is None:
        return (signal + product("td,de->te", active, output_weight), totals)
    out_grad = upstream.astype(jnp.bfloat16)
    grad_output = product("td,te->de", active, out_grad)
    grad_active = product("te,de->td", out_grad, output_weight)
    grad_bn = silu_pull(grad_active)[0]
    grad_mixed, grad_average, grad_inverse, grad_scale, grad_shift = apply_pull(grad_bn)
    grad_average, grad_inverse = lax.psum((grad_average, grad_inverse), ("dp", "fsdp"))
    grad_first, grad_second = moment_pull((grad_average, grad_inverse))
    grad_mixed = grad_mixed + frame_mask * (grad_first + 2.0 * mixed * grad_second)
    grad_gated, grad_kernel = conv_pull(grad_mixed)
    grad_joined = gate_pull(grad_gated * frame_mask)[0].astype(jnp.bfloat16)
    grad_gating = product("td,te->de", normed, grad_joined)
    grad_normed = product("te,de->td", grad_joined, gating_weight)
    grad_signal, grad_gain = norm_pull(grad_normed)
    return (
        upstream + grad_signal,
        (grad_gain, grad_gating, grad_kernel, grad_scale, grad_shift, grad_output),
    )


def any_layer(
    tokens,
    lengths,
    cotangent,
    early_norm,
    early_up,
    early_down,
    attend_norm,
    heads_weight,
    position_weight,
    content_bias,
    position_bias,
    attend_output,
    mixer_norm,
    gating_weight,
    depth_kernel,
    batch_gain,
    batch_shift,
    mixer_output,
    late_norm,
    late_up,
    late_down,
    final_gain,
):
    utterances = lengths.shape[0]
    frames = tokens.shape[0] // utterances
    key_valid = lax.iota(jnp.int32, frames)[None, :] < lengths[:, None]
    frame_mask = key_valid.reshape(-1, 1).astype(jnp.float32)
    table = distances(frames, tokens.shape[1]).astype(jnp.bfloat16)
    start = tokens.astype(jnp.float32)
    early = prepare_ffn(early_norm, early_up, early_down)
    after_early = ffn_forward(start, early)
    attend = gather_attend(
        attend_norm,
        heads_weight,
        position_weight,
        content_bias,
        position_bias,
        attend_output,
        final_gain,
    )
    after_attend = attend_block(after_early, attend, key_valid, table, None)
    mixer = gather_mixer(
        mixer_norm, gating_weight, depth_kernel, batch_gain, batch_shift, mixer_output
    )
    after_mixer, totals = mixer_block(after_attend, mixer, frame_mask, frames, None, None)
    late = prepare_ffn(late_norm, late_up, late_down)
    after_late = ffn_forward(after_mixer, late)
    output, final_pull = jax.vjp(layer_norm, after_late, attend[6].astype(jnp.float32))
    upstream, grad_final = final_pull(cotangent.astype(jnp.float32) * frame_mask)
    late_back = prepare_ffn(late_norm, late_up, late_down)
    upstream, late_shards = ffn_backward(after_mixer, late_back, upstream)
    mixer_back = gather_mixer(
        mixer_norm, gating_weight, depth_kernel, batch_gain, batch_shift, mixer_output
    )
    upstream, mixer_grads = mixer_block(
        after_attend, mixer_back, frame_mask, frames, totals, upstream
    )
    attend_back = gather_attend(
        attend_norm,
        heads_weight,
        position_weight,
        content_bias,
        position_bias,
        attend_output,
        final_gain,
    )
    upstream, attend_grads = attend_block(after_early, attend_back, key_valid, table, upstream)
    middle = (
        lax.psum_scatter(
            attend_grads[0].astype(jnp.bfloat16), "fsdp", scatter_dimension=0, tiled=True
        ).astype(jnp.float32),
        lax.psum_scatter(
            attend_grads[1].astype(jnp.bfloat16), "fsdp", scatter_dimension=0, tiled=True
        ).astype(jnp.float32),
        lax.psum_scatter(
            attend_grads[2].astype(jnp.bfloat16), "fsdp", scatter_dimension=0, tiled=True
        ).astype(jnp.float32),
        lax.psum_scatter(
            attend_grads[3].astype(jnp.bfloat16), "fsdp", scatter_dimension=0, tiled=True
        ).astype(jnp.float32),
        lax.psum_scatter(
            attend_grads[4].astype(jnp.bfloat16), "fsdp", scatter_dimension=0, tiled=True
        ).astype(jnp.float32),
        lax.psum_scatter(
            attend_grads[5].astype(jnp.bfloat16), "fsdp", scatter_dimension=0, tiled=True
        ).astype(jnp.float32),
        lax.psum_scatter(
            mixer_grads[0].astype(jnp.bfloat16), "fsdp", scatter_dimension=0, tiled=True
        ).astype(jnp.float32),
        lax.psum_scatter(
            mixer_grads[1].astype(jnp.bfloat16), "fsdp", scatter_dimension=0, tiled=True
        ).astype(jnp.float32),
        lax.psum_scatter(
            mixer_grads[2].astype(jnp.bfloat16), "fsdp", scatter_dimension=1, tiled=True
        ).astype(jnp.float32),
        lax.psum_scatter(
            mixer_grads[3].astype(jnp.bfloat16), "fsdp", scatter_dimension=0, tiled=True
        ).astype(jnp.float32),
        lax.psum_scatter(
            mixer_grads[4].astype(jnp.bfloat16), "fsdp", scatter_dimension=0, tiled=True
        ).astype(jnp.float32),
        lax.psum_scatter(
            mixer_grads[5].astype(jnp.bfloat16), "fsdp", scatter_dimension=0, tiled=True
        ).astype(jnp.float32),
        lax.psum_scatter(
            grad_final.astype(jnp.bfloat16), "fsdp", scatter_dimension=0, tiled=True
        ).astype(jnp.float32),
    )
    early_back = prepare_ffn(early_norm, early_up, early_down)
    upstream, early_shards = ffn_backward(start, early_back, upstream)
    summed = (
        lax.psum(early_shards[0].astype(jnp.bfloat16), "dp").astype(jnp.float32),
        lax.psum(early_shards[1].astype(jnp.bfloat16), "dp").astype(jnp.float32),
        lax.psum(early_shards[2].astype(jnp.bfloat16), "dp").astype(jnp.float32),
        lax.psum(middle[0].astype(jnp.bfloat16), "dp").astype(jnp.float32),
        lax.psum(middle[1].astype(jnp.bfloat16), "dp").astype(jnp.float32),
        lax.psum(middle[2].astype(jnp.bfloat16), "dp").astype(jnp.float32),
        lax.psum(middle[3].astype(jnp.bfloat16), "dp").astype(jnp.float32),
        lax.psum(middle[4].astype(jnp.bfloat16), "dp").astype(jnp.float32),
        lax.psum(middle[5].astype(jnp.bfloat16), "dp").astype(jnp.float32),
        lax.psum(middle[6].astype(jnp.bfloat16), "dp").astype(jnp.float32),
        lax.psum(middle[7].astype(jnp.bfloat16), "dp").astype(jnp.float32),
        lax.psum(middle[8].astype(jnp.bfloat16), "dp").astype(jnp.float32),
        lax.psum(middle[9].astype(jnp.bfloat16), "dp").astype(jnp.float32),
        lax.psum(middle[10].astype(jnp.bfloat16), "dp").astype(jnp.float32),
        lax.psum(middle[11].astype(jnp.bfloat16), "dp").astype(jnp.float32),
        lax.psum(late_shards[0].astype(jnp.bfloat16), "dp").astype(jnp.float32),
        lax.psum(late_shards[1].astype(jnp.bfloat16), "dp").astype(jnp.float32),
        lax.psum(late_shards[2].astype(jnp.bfloat16), "dp").astype(jnp.float32),
        lax.psum(middle[12].astype(jnp.bfloat16), "dp").astype(jnp.float32),
    )
    return (
        output.astype(jnp.bfloat16),
        upstream.astype(jnp.bfloat16),
        summed[0],
        summed[1],
        summed[2],
        summed[3],
        summed[4],
        summed[5],
        summed[6],
        summed[7],
        summed[8],
        summed[9],
        summed[10],
        summed[11],
        summed[12],
        summed[13],
        summed[14],
        summed[15],
        summed[16],
        summed[17],
        summed[18],
    )


def pair_mesh(mesh):
    if dict(mesh.shape) != {"dp": 16, "fsdp": 2}:
        return None
    return Mesh(mesh.devices.reshape(4, 2, 2, 2), PairPlan.axes)


def spec(mesh, *dims):
    names = {"dp": ("z", "y", "c"), "fsdp": ("x",)}
    if "dp" in mesh.shape:
        names = {"dp": ("dp",), "fsdp": ("fsdp",)}
    return P(*[None if dim is None else sum((names[d] for d in dim), ()) for dim in dims])


def solution(mesh):
    inner = pair_mesh(mesh)
    layer = any_layer if inner is None else pair_layer
    inner = mesh if inner is None else inner
    all_rows, vector = spec(inner, ("dp", "fsdp"), None), spec(inner, ("fsdp",))
    by_rows, by_cols = spec(inner, ("fsdp",), None), spec(inner, None, ("fsdp",))
    weights = (
        vector,
        by_cols,
        by_rows,
        vector,
        by_rows,
        by_rows,
        vector,
        vector,
        by_rows,
        vector,
        by_rows,
        by_cols,
        vector,
        vector,
        by_rows,
        vector,
        by_cols,
        by_rows,
        vector,
    )
    return jax.shard_map(
        layer,
        mesh=inner,
        in_specs=(all_rows, spec(inner, ("dp", "fsdp")), all_rows) + weights,
        out_specs=(all_rows, all_rows) + weights,
        check_vma=False,
    )
```
